512 devices in a mesh: seq: 32 (over z, core), dp: 16 (over x, y).
Axes of the slice: x: 4, y: 4, z: 16, core: 2. Of those that a mesh axis runs over, the one named last changes fastest.
Arguments:
- queries: bfloat16 [16, 5120, 2048], P('dp', 'seq'), may hold values from -6 to 6
- keys: bfloat16 [16, 5120, 2048], P('dp', 'seq'), may hold values from -6 to 6
- values: bfloat16 [16, 5120, 2048], P('dp', 'seq'), may hold values from -6 to 6
- keep: int32 [16, 5120, 2048], P('dp', 'seq'), may hold values 0 or 1
- gain: float32 [2048], replicated, may hold values from 0.25 to 1.75
- out_weight: bfloat16 [2048, 2048], P(None, 'dp'), may hold values from -0.125 to 0.125
Outputs:
- projected: bfloat16 [16, 5120, 2048], P('dp', 'seq')
The draws below stay inside these ranges and needn't reach their ends.
All inputs are finite; a program needn't handle non-finite values. No bound on the sum of `keep` on one device may be relied on, other than what follows from the above.
Results may differ from the reference program's by a relative error of at most 0.0051.
Values may be sent and summed in bfloat16 or wider, within the bound.
No kernel may reach another device: no remote copies, remote signals or barrier semaphores. Data moves between devices by JAX's collectives and lax.ppermute only.
A program may use at most 128 MiB of HBM per device.

```python
import jax
import jax.numpy as jnp
from jax import lax

HEADS = 16
HEAD = 128
DOUT = 2048
TOK_DEV = 160
HC = 2048
TOKENS = 5120
WINDOWS = 16
N_SEQ = 32


def plant(entries, rng, low, high):
    spot = [jax.random.randint(jax.random.fold_in(rng, axis), (), 0, length) for axis, length in enumerate(entries.shape)]
    main_axis = entries.shape.index(max(entries.shape))
    beside = spot[:main_axis] + [(spot[main_axis] + 1) % entries.shape[main_axis]] + spot[main_axis + 1:]
    return entries.at[tuple(spot)].set(low).at[tuple(beside)].set(high)


def level_of(rng, extent, shards, least, top_value):
    level, own = 1.0, jax.random.fold_in(rng, 6)
    for position, blocks in shards:
        draws = jnp.exp(jax.random.uniform(jax.random.fold_in(own, position), (blocks,), jnp.float32, least / len(shards), top_value / len(shards)))
        level = level * jnp.repeat(draws, extent[position] // blocks).reshape([-1 if axis == position else 1 for axis in range(len(extent))])
    return level


def noise(key, shape, spread, most, pieces=(), held_as=jnp.bfloat16):
    drawn = spread * jax.random.normal(key, shape, jnp.float32)
    if pieces:
        drawn = drawn * level_of(key, shape, pieces, -0.22, 0.18)
    return jnp.clip(drawn, -most, most).astype(held_as)


def setup_inputs(seed: int = 0) -> dict:
    splits = jax.random.split(jax.random.key(seed), 7)
    queries = noise(splits[0], (WINDOWS, TOKENS, HC), 1.0, 6.0, ((0, 16), (1, 32)))
    keys = noise(splits[1], (WINDOWS, TOKENS, HC), 1.0, 6.0, ((0, 16), (1, 32)))
    values = noise(splits[2], (WINDOWS, TOKENS, HC), 1.0, 6.0, ((0, 16), (1, 32)))
    keep = plant((jax.random.randint(splits[3], (WINDOWS, TOKENS, HC), 0, 10) < 9).astype(jnp.int32), jax.random.fold_in(splits[3], 1), 0, 1)
    gain = jnp.clip(1.0 + 0.15 * jax.random.normal(splits[4], (HC,), jnp.float32), 0.25, 1.75)
    out_weight = noise(splits[5], (HC, DOUT), HC ** -0.5, 0.125, ((1, 16),))
    return dict(queries=queries, keys=keys, values=values, keep=keep, gain=gain, out_weight=out_weight)


def feature(x):
    xf = x.astype(jnp.float32)
    return jnp.where(xf > 0, xf + 1.0, jnp.exp(jnp.minimum(xf, 0.0))).astype(jnp.bfloat16)

def reference(queries, keys, values, keep, gain, out_weight):
    causal = (jnp.arange(TOK_DEV)[:, None] >= jnp.arange(TOK_DEV)[None, :]).astype(jnp.float32)
    gain_heads = gain.reshape(HEADS, HEAD)

    def window(items):
        q_win, k_win, v_win, keep_win = items
        fq = feature(q_win).reshape(N_SEQ, TOK_DEV, HEADS, HEAD)
        fk = feature(k_win).reshape(N_SEQ, TOK_DEV, HEADS, HEAD)
        vv = v_win.reshape(N_SEQ, TOK_DEV, HEADS, HEAD)
        states = jnp.einsum('bthc,bthd->bhcd', fk.astype(jnp.float32), vv.astype(jnp.float32))
        running = jnp.cumsum(states, axis=0)
        prefix = jnp.concatenate([jnp.zeros_like(states[:1]), running[:-1]], axis=0).astype(jnp.bfloat16)

        def block(parts):
            fqb, fkb, vb, pb = parts
            inter = jnp.einsum('thc,hcd->thd', fqb.astype(jnp.float32), pb.astype(jnp.float32))
            scores = jnp.einsum('thc,shc->hts', fqb.astype(jnp.float32), fkb.astype(jnp.float32))
            scores = (scores * causal[None]).astype(jnp.bfloat16)
            intra = jnp.einsum('hts,shd->thd', scores.astype(jnp.float32), vb.astype(jnp.float32))
            return inter + intra
        numer = lax.map(block, (fq, fk, vv, prefix)).reshape(TOKENS, HEADS, HEAD)
        normed = numer * lax.rsqrt(lax.optimization_barrier(jnp.mean(numer * numer, axis=-1, keepdims=True)) + 1e-06) * gain_heads
        mask = keep_win.reshape(TOKENS, HEADS, HEAD).astype(jnp.float32)
        dropped = (normed * mask * (1.0 / 0.9)).astype(jnp.bfloat16).reshape(TOKENS, HEADS * HEAD)
        return jnp.dot(dropped, out_weight, preferred_element_type=jnp.float32).astype(jnp.bfloat16)
    return lax.map(window, (queries, keys, values, keep))
```

```python
import jax
import jax.numpy as jnp
import numpy as np
from jax import lax
from jax.experimental import pallas as pl
from jax.experimental.pallas import tpu as pltpu
from jax.sharding import PartitionSpec as P

HEADS = 16
HEAD = 128
HALF = 8
TOK = 160
HC = 2048
F32 = jnp.float32
BF16 = jnp.bfloat16
SWAP = [(0, 1), (1, 0)]


def feature(x):
    xf = x.astype(F32)
    return jnp.where(xf > 0, xf + 1.0, jnp.exp(jnp.minimum(xf, 0.0))).astype(BF16)


def dot(a, b, contract):
    return lax.dot_general(a, b, (contract, ((), ())), preferred_element_type=F32)


def state_kernel(core, k, v, send, own):
    step = pl.program_id(0)
    for h in range(4):
        cols = slice(h * HEAD, (h + 1) * HEAD)
        s = dot(feature(k[:, cols]), v[:, cols], ((0,), (0,)))

        @pl.when(step < 2)
        def _():
            send[h] = s.astype(BF16)

        @pl.when(step >= 2)
        def _():
            own[h] = s


def block_states(core, keys, values):
    def half(i, core):
        return jnp.where(i < 2, 1 - core[0], core[0]) * 2 + i % 2

    spec = pl.BlockSpec((TOK, 512), lambda i, core: (0, half(i, core)))
    return pl.pallas_call(
        state_kernel,
        grid_spec=pltpu.PrefetchScalarGridSpec(
            num_scalar_prefetch=1,
            grid=(4,),
            in_specs=[spec, spec],
            out_specs=[
                pl.BlockSpec((4, HEAD, HEAD), lambda i, core: (jnp.minimum(i, 1), 0, 0)),
                pl.BlockSpec((4, HEAD, HEAD), lambda i, core: (jnp.maximum(i - 2, 0), 0, 0)),
            ],
        ),
        out_shape=[
            jax.ShapeDtypeStruct((HALF, HEAD, HEAD), BF16),
            jax.ShapeDtypeStruct((HALF, HEAD, HEAD), F32),
        ],
        name="block_states",
    )(core, keys, values)


def scan_kernel(x, y):
    run = jnp.zeros(x.shape[1:], F32)
    for z in range(x.shape[0]):
        y[z] = run.astype(BF16)
        run = run + x[z].astype(F32)


def scan_chips(x):
    return pl.pallas_call(scan_kernel, out_shape=jax.ShapeDtypeStruct(x.shape, BF16), name="scan_chips")(x)


def heads_kernel(core, q, k, v, keep, gain, mine, theirs, out):
    step = pl.program_id(0)
    row = lax.broadcasted_iota(jnp.int32, (TOK, TOK), 0)
    col = lax.broadcasted_iota(jnp.int32, (TOK, TOK), 1)
    causal = row >= col
    for h in range(4):
        cols = slice(h * HEAD, (h + 1) * HEAD)
        fq = feature(q[:, cols])
        fk = feature(k[:, cols])
        prefix = jnp.where(step < 2, mine[h].astype(F32), theirs[h].astype(F32)).astype(BF16)
        scores = dot(fq, fk, ((1,), (1,)))
        scores = jnp.where(causal, scores, 0.0).astype(BF16)
        numer = dot(fq, prefix, ((1,), (0,))) + dot(scores, v[:, cols], ((1,), (0,)))
        mean = jnp.mean(numer * numer, axis=-1, keepdims=True)
        normed = numer * lax.rsqrt(mean + 1e-06) * gain[:, cols]
        out[:, cols] = (normed * keep[:, cols].astype(F32) * (1.0 / 0.9)).astype(BF16)


def heads(core, q, k, v, keep, gain, mine, theirs):
    def half(i, core):
        return jnp.where(i < 2, core[0], 1 - core[0]) * 2 + i % 2

    spec = pl.BlockSpec((TOK, 512), lambda i, core: (0, half(i, core)))
    state = pl.BlockSpec((4, HEAD, HEAD), lambda i, core: (i % 2, 0, 0))
    return pl.pallas_call(
        heads_kernel,
        grid_spec=pltpu.PrefetchScalarGridSpec(
            num_scalar_prefetch=1,
            grid=(4,),
            in_specs=[spec, spec, spec, spec, pl.BlockSpec((1, 512), lambda i, core: (0, half(i, core))), state, state],
            out_specs=spec,
        ),
        out_shape=jax.ShapeDtypeStruct((TOK, HC), BF16),
        name="heads",
    )(core, q, k, v, keep, gain, mine, theirs)


def project_kernel(x, top, bottom, out):
    acc = dot(x[:, : HC // 2], top[...], ((1,), (0,)))
    acc += dot(x[:, HC // 2 :], bottom[...], ((1,), (0,)))
    out[...] = acc.astype(BF16)


def project(dropped, weight):
    wide = 512
    return pl.pallas_call(
        project_kernel,
        grid=(HC // wide,),
        in_specs=[
            pl.BlockSpec((TOK, HC), lambda i: (0, 0)),
            pl.BlockSpec((HC // 2, wide), lambda i: (0, i)),
            pl.BlockSpec((HC // 2, wide), lambda i: (0, i + HC // wide)),
        ],
        out_specs=pl.BlockSpec((TOK, wide), lambda i: (0, i)),
        out_shape=jax.ShapeDtypeStruct((TOK, HC), BF16),
        name="project",
    )(dropped, weight, weight)


def on_device(queries, keys, values, keep, gain, out_weight):
    place = lax.axis_index("core")
    core = place.astype(jnp.int32).reshape(1)
    part = lax.dynamic_slice_in_dim(out_weight, place * (HC // 2), HC // 2, 0)
    weight = lax.all_gather(part, ("core", "x", "y"), axis=1, tiled=True)

    send, own = block_states(core, keys[0], values[0])
    other = lax.ppermute(send, "core", SWAP)
    chip = (own + other.astype(F32)).astype(BF16).reshape(16, HEAD // 2, HEAD)
    slices = lax.all_to_all(chip, "z", 0, 0)
    before = lax.all_to_all(scan_chips(slices), "z", 0, 0).reshape(HALF, HEAD, HEAD)
    before = before.astype(F32)
    first = place == 0
    there = (before + jnp.where(first, own, 0.0)).astype(BF16)
    mine = (before + jnp.where(first, 0.0, other.astype(F32))).astype(BF16)
    theirs = lax.ppermute(there, "core", SWAP)
    dropped = heads(core, queries[0], keys[0], values[0], keep[0], gain.reshape(1, HC), mine, theirs)
    return project(dropped, weight)[None]


def solution(mesh):
    fine = jax.sharding.Mesh(np.asarray(mesh.devices).reshape(16, 2, 4, 4), ("z", "core", "x", "y"))
    tokens = P(("x", "y"), ("z", "core"), None)
    return jax.shard_map(
        on_device,
        mesh=fine,
        in_specs=(tokens, tokens, tokens, tokens, P(), P(None, ("x", "y"))),
        out_specs=tokens,
        check_vma=False,
    )
```

```python
import jax
import jax.numpy as jnp
import numpy as np
from jax import lax
from jax.experimental import pallas as pl
from jax.experimental.pallas import tpu as pltpu
from jax.sharding import PartitionSpec as P

HEAD = 128
HALF = 8
TOK = 160
HC = 2048
F32 = jnp.float32
BF16 = jnp.bfloat16
SWAP = [(0, 1), (1, 0)]
UP = [(i, (i + 1) % 4) for i in range(4)]
DOWN = [(i, (i + 3) % 4) for i in range(4)]


def feature(x):
    xf = x.astype(F32)
    return jnp.where(xf > 0, xf + 1.0, jnp.exp(jnp.minimum(xf, 0.0))).astype(BF16)


def dot(a, b, contract):
    return lax.dot_general(a, b, (contract, ((), ())), preferred_element_type=F32)


def cost(flops, moved):
    return pl.CostEstimate(flops=flops, bytes_accessed=moved, transcendentals=0)


def state_kernel(core, k, v, send, own):
    step = pl.program_id(0)

    def state(h):
        cols = slice(h * HEAD, (h + 1) * HEAD)
        return dot(feature(k[:, cols]), v[:, cols], ((0,), (0,)))

    @pl.when(step < 2)
    def _():
        for h in range(4):
            send[h] = state(h).astype(BF16)

    @pl.when(step >= 2)
    def _():
        for h in range(4):
            own[h] = state(h)


def block_states(core, keys, values):
    def half(i, core):
        return jnp.where(i < 2, 1 - core[0], core[0]) * 2 + i % 2

    spec = pl.BlockSpec((TOK, 512), lambda i, core: (0, half(i, core)))
    return pl.pallas_call(
        state_kernel,
        grid_spec=pltpu.PrefetchScalarGridSpec(
            num_scalar_prefetch=1,
            grid=(4,),
            in_specs=[spec, spec],
            out_specs=[
                pl.BlockSpec((4, HEAD, HEAD), lambda i, core: (jnp.minimum(i, 1), 0, 0)),
                pl.BlockSpec((4, HEAD, HEAD), lambda i, core: (jnp.maximum(i - 2, 0), 0, 0)),
            ],
        ),
        out_shape=[
            jax.ShapeDtypeStruct((HALF, HEAD, HEAD), BF16),
            jax.ShapeDtypeStruct((HALF, HEAD, HEAD), F32),
        ],
        cost_estimate=cost(84_000_000, 2_000_000),
        name="block_states",
    )(core, keys, values)


def scan_kernel(x, y):
    run = jnp.zeros(x.shape[1:], F32)
    for z in range(x.shape[0]):
        y[z] = run.astype(BF16)
        run = run + x[z].astype(F32)


def scan_chips(x):
    return pl.pallas_call(
        scan_kernel,
        out_shape=jax.ShapeDtypeStruct(x.shape, BF16),
        cost_estimate=cost(200_000, 500_000),
        name="scan_chips",
    )(x)


def intra_kernel(q, k, v, intra, fq):
    row = lax.broadcasted_iota(jnp.int32, (TOK, TOK), 0)
    col = lax.broadcasted_iota(jnp.int32, (TOK, TOK), 1)
    causal = row >= col
    for h in range(4):
        cols = slice(h * HEAD, (h + 1) * HEAD)
        fqh = feature(q[:, cols])
        scores = dot(fqh, feature(k[:, cols]), ((1,), (1,)))
        scores = jnp.where(causal, scores, 0.0).astype(BF16)
        intra[:, cols] = dot(scores, v[:, cols], ((1,), (0,)))
        fq[:, cols] = fqh


def intra_block(q, k, v):
    spec = pl.BlockSpec((TOK, 512), lambda i: (0, i))
    return pl.pallas_call(
        intra_kernel,
        grid=(4,),
        in_specs=[spec] * 3,
        out_specs=[spec] * 2,
        out_shape=[jax.ShapeDtypeStruct((TOK, HC), F32), jax.ShapeDtypeStruct((TOK, HC), BF16)],
        cost_estimate=cost(210_000_000, 4_000_000),
        name="intra_block",
    )(q, k, v)


def heads_kernel(core, fq, intra, keep, gain, mine, theirs, out):
    step = pl.program_id(0)
    for h in range(4):
        cols = slice(h * HEAD, (h + 1) * HEAD)
        prefix = jnp.where(step < 2, mine[h].astype(F32), theirs[h].astype(F32)).astype(BF16)
        numer = dot(fq[:, cols], prefix, ((1,), (0,))) + intra[:, cols]
        mean = jnp.mean(numer * numer, axis=-1, keepdims=True)
        normed = numer * lax.rsqrt(mean + 1e-06) * gain[:, cols]
        out[:, cols] = (normed * keep[:, cols].astype(F32) * (1.0 / 0.9)).astype(BF16)


def heads(core, fq, intra, keep, gain, mine, theirs):
    def half(i, core):
        return jnp.where(i < 2, core[0], 1 - core[0]) * 2 + i % 2

    spec = pl.BlockSpec((TOK, 512), lambda i, core: (0, half(i, core)))
    state = pl.BlockSpec((4, HEAD, HEAD), lambda i, core: (i % 2, 0, 0))
    return pl.pallas_call(
        heads_kernel,
        grid_spec=pltpu.PrefetchScalarGridSpec(
            num_scalar_prefetch=1,
            grid=(4,),
            in_specs=[spec, spec, spec, pl.BlockSpec((1, 512), lambda i, core: (0, half(i, core))), state, state],
            out_specs=spec,
        ),
        out_shape=jax.ShapeDtypeStruct((TOK, HC), BF16),
        cost_estimate=cost(90_000_000, 5_000_000),
        name="heads",
    )(core, fq, intra, keep, gain, mine, theirs)


def project_kernel(place, x, *refs):
    own, other, out = refs[:4], refs[4:8], refs[8]
    half = HC // 2
    low = x[:, pl.ds(pl.multiple_of(place[0] * half, half), half)]
    high = x[:, pl.ds(pl.multiple_of((1 - place[0]) * half, half), half)]
    for a in (0, 2):
        acc = dot(low, jnp.concatenate([own[a][0], own[a + 1][0]], axis=1), ((1,), (0,)))
        acc += dot(high, jnp.concatenate([other[a][0], other[a + 1][0]], axis=1), ((1,), (0,)))
        for b in (0, 1):
            at = pl.multiple_of((place[2] + 4 - a - b) % 4 * HEAD, HEAD)
            out[:, pl.ds(at, HEAD)] = acc[:, b * HEAD : (b + 1) * HEAD].astype(BF16)


def project(place, dropped, own, other):
    piece = pl.BlockSpec((1, HC // 2, HEAD), lambda i, place: (i, 0, 0))
    return pl.pallas_call(
        project_kernel,
        grid_spec=pltpu.PrefetchScalarGridSpec(
            num_scalar_prefetch=1,
            grid=(4,),
            in_specs=[pl.BlockSpec((TOK, HC), lambda i, place: (0, 0))] + [piece] * 8,
            out_specs=pl.BlockSpec((TOK, 512), lambda i, place: (0, (place[1] + 4 - i) % 4)),
        ),
        out_shape=jax.ShapeDtypeStruct((TOK, HC), BF16),
        cost_estimate=cost(1_340_000_000, 10_000_000),
        name="project",
    )(place, dropped, *own, *other)


def swap(x):
    return lax.ppermute(x, "core", SWAP)


def on_device(queries, keys, values, keep, gain, out_weight):
    core = lax.axis_index("core")
    place = jnp.stack([core, lax.axis_index("x"), lax.axis_index("y")]).astype(jnp.int32)

    part = lax.dynamic_slice_in_dim(out_weight, core * (HC // 2), HC // 2, 0)
    x1 = lax.ppermute(part, "x", UP)
    x3 = lax.ppermute(part, "x", DOWN)
    send, own = block_states(place, keys[0], values[0])
    x1, send, own = lax.optimization_barrier((x1, send, own))
    x2 = lax.ppermute(x1, "x", UP)
    row = jnp.stack([part, x1, x2, x3])
    y1 = lax.ppermute(row, "y", UP)
    y3 = lax.ppermute(row, "y", DOWN)
    y2 = lax.ppermute(y1, "y", UP)

    other = swap(send)
    chip = (own + other.astype(F32)).astype(BF16).reshape(16, HEAD // 2, HEAD)
    slices = lax.all_to_all(chip, "z", 0, 0)
    intra, fq = intra_block(queries[0], keys[0], values[0])
    slices, intra, fq = lax.optimization_barrier((slices, intra, fq))
    before = lax.all_to_all(scan_chips(slices), "z", 0, 0).reshape(HALF, HEAD, HEAD)
    before = before.astype(F32)
    first = core == 0
    there = (before + jnp.where(first, own, 0.0)).astype(BF16)
    mine = (before + jnp.where(first, 0.0, other.astype(F32))).astype(BF16)
    theirs = swap(there)
    dropped = heads(place, fq, intra, keep[0], gain.reshape(1, HC), mine, theirs)
    mine_w = (row, y1, y2, y3)
    return project(place, dropped, mine_w, tuple(swap(w) for w in mine_w))[None]


def solution(mesh):
    fine = jax.sharding.Mesh(np.asarray(mesh.devices).reshape(16, 2, 4, 4), ("z", "core", "x", "y"))
    tokens = P(("x", "y"), ("z", "core"), None)
    return jax.shard_map(
        on_device,
        mesh=fine,
        in_specs=(tokens, tokens, tokens, tokens, P(), P(None, ("x", "y"))),
        out_specs=tokens,
        check_vma=False,
    )
```
